32 devices in a mesh: gx: 4 (over y, core), gy: 8 (over z, x).
Axes of the slice: x: 2, y: 2, z: 4, core: 2. Of those that a mesh axis runs over, the one named last changes fastest.
Arguments:
- points: float32 [8192, 512], P(('gx', 'gy')), may hold values from -6 to 6
- upstream: float32 [8192, 512], P(('gx', 'gy')), may hold values from -6 to 6
- gains: float32 [2, 512], replicated, may hold values from 0.1 to 1.9
- w_qkv: float32 [2, 512, 1536], replicated, may hold values from -20 to 20
- w_proj: float32 [2, 512, 512], replicated, may hold values from -0.25 to 0.25
- z_route: int32 [512, 2], P(('gx', 'gy')), may hold values from 0 to 31, as said below
- h_route: int32 [512, 2], P(('gx', 'gy')), may hold values from 0 to 31, as said below
Outputs:
- point_grad: float32 [8192, 512], P(('gx', 'gy'))
- gain_grad: float32 [2, 512], P(None, ('gx', 'gy'))
- qkv_grad: float32 [2, 512, 1536], P(None, ('gx', 'gy'))
- proj_grad: float32 [2, 512, 512], P(None, ('gx', 'gy'))
The draws below stay inside these ranges and needn't reach their ends.
Inputs may be any that keep to these rules, and one draw needn't show every extreme that they name: `z_route`: column 0 names the owner device (gx index times 8 plus gy index), which has the same gx index as the device that holds the segment; column 1 names the slot at the owner, below 16. Every slot of every device is named exactly once, and each device sends exactly 2 of its segments to each owner of its gx index. `h_route`: column 0 names the owner device (gx index times 8 plus gy index), which has the same gy index as the device that holds the segment; column 1 names the slot at the owner, below 16. Every slot of every device is named exactly once, and each device sends exactly 4 of its segments to each owner of its gy index.
All inputs are finite; a program needn't handle non-finite values.
Results may differ from the reference program's by a relative error of at most 0.00085.
Values sent between devices are 32-bit elements; how exact they have to be, the bound alone decides.
A program may use at most 128 MiB of HBM per device.

```python
import math
import jax
import jax.numpy as jnp
from jax import lax

D = 512
HEADS = 32
PATCH = 128
SEG = 16
SEG_DEV = 16
TOKENS = 8192
N_GX = 4
N_GY = 8


def regular_routes(key, groups, group_size, per_holder):
    per_pair = per_holder // group_size

    def one_group(group_key):
        subkeys = jax.random.split(group_key, 4)
        holder_perms = jax.vmap(lambda k: jax.random.permutation(k, per_holder))(jax.random.split(subkeys[0], group_size))
        holder_rank = jax.vmap(lambda k: jax.random.permutation(k, group_size))(jax.random.split(subkeys[1], group_size))
        slot_perms = jax.vmap(lambda k: jax.random.permutation(k, per_holder))(jax.random.split(subkeys[2], group_size))
        rename = jax.random.permutation(subkeys[3], group_size)
        owner_raw = holder_perms % group_size
        occurrence = holder_perms // group_size
        holder = jnp.arange(group_size)[:, None]
        rank_here = holder_rank[owner_raw, holder]
        slot_index = slot_perms[owner_raw, rank_here * per_pair + occurrence]
        return (rename[owner_raw], slot_index)
    return jax.vmap(one_group)(jax.random.split(key, groups))


def draw_z_route(key, part):
    owner_local, slot_index = regular_routes(jax.random.fold_in(key, 11), N_GX, N_GY, SEG_DEV)
    group_index = jnp.arange(N_GX)[:, None, None]
    owners = group_index * N_GY + owner_local
    return jnp.stack([owners.reshape(-1), slot_index.reshape(-1)], axis=1).astype(jnp.int32)


def draw_h_route(key, part):
    owner_local, slot_index = regular_routes(jax.random.fold_in(key, 23), N_GY, N_GX, SEG_DEV)
    owner_local = jnp.transpose(owner_local, (1, 0, 2))
    slot_index = jnp.transpose(slot_index, (1, 0, 2))
    group_index = jnp.arange(N_GY)[None, :, None]
    owners = owner_local * N_GY + group_index
    return jnp.stack([owners.reshape(-1), slot_index.reshape(-1)], axis=1).astype(jnp.int32)


def draw_w_qkv(key, part):
    base = jax.random.normal(key, (2, D, 3 * D), jnp.float32) * (1.0 / math.sqrt(D))
    return base.astype(jnp.float32)


def shard_levels(key, shape, cuts, smallest, largest):
    gain = 1.0
    for axis_at, blocks in cuts:
        steps = jax.random.uniform(jax.random.fold_in(jax.random.fold_in(key, 6), axis_at), (blocks,), jnp.float32, smallest / len(cuts), largest / len(cuts))
        gain = gain * jnp.repeat(jnp.exp(steps), shape[axis_at] // blocks).reshape((-1,) + (1,) * (len(shape) - 1 - axis_at))
    return gain


def normal_values(own_key, dims, width, limit, shards=(), kind=jnp.bfloat16):
    result = jax.random.normal(own_key, dims, jnp.float32) * width
    if len(shards) > 0:
        result = shard_levels(own_key, dims, shards, -0.22, 0.18) * result
    return jnp.clip(result, min=-limit, max=limit).astype(kind)


def setup_inputs(seed: int = 0) -> dict:
    key_of = jax.random.split(jax.random.key(seed), 8)
    return {
        "points": normal_values(key_of[0], (TOKENS, D), 1.0, 6.0, ((0, 32),), jnp.float32),
        "upstream": normal_values(key_of[1], (TOKENS, D), 1.0, 6.0, ((0, 32),), jnp.float32),
        "gains": jnp.clip(1.0 + 0.18 * jax.random.normal(key_of[2], (2, D), jnp.float32), 0.1, 1.9),
        "w_qkv": draw_w_qkv(jax.random.fold_in(key_of[7], 71), 0),
        "w_proj": normal_values(key_of[4], (2, D, D), D ** -0.5, 0.25, (), jnp.float32),
        "z_route": draw_z_route(jax.random.fold_in(key_of[7], 71), 0),
        "h_route": draw_h_route(jax.random.fold_in(key_of[7], 71), 0),
    }


exact_mode = lax.Precision.HIGHEST
epsilon = 1e-05

def patch_attend(patch_rows):
    head_dim = D // HEADS
    queries = patch_rows[:, 0]
    key_rows = patch_rows[:, 1]
    value_rows = patch_rows[:, 2]
    scores = jnp.einsum('ihd,jhd->hij', queries, key_rows, precision=exact_mode) * (1.0 / math.sqrt(head_dim))
    attention = jax.nn.softmax(scores, axis=-1)
    mixed_rows = jnp.einsum('hij,jhd->ihd', attention, value_rows, precision=exact_mode)
    return mixed_rows.reshape(PATCH, D)

def attend_block(rows_in, gain_row, qkv_weight, proj_weight):
    row_count = rows_in.shape[0]
    row_mean = lax.optimization_barrier(jnp.mean(rows_in, axis=-1, keepdims=True))
    centered = rows_in - row_mean
    row_var = lax.optimization_barrier(jnp.mean(centered * centered, axis=-1, keepdims=True))
    normed = centered * lax.rsqrt(row_var + epsilon) * gain_row
    projected = jnp.dot(normed, qkv_weight, precision=exact_mode)
    projected = projected.reshape(row_count // PATCH, PATCH, 3, HEADS, D // HEADS)
    mixed_rows = lax.map(jax.checkpoint(patch_attend), projected)
    return rows_in + jnp.dot(mixed_rows.reshape(row_count, D), proj_weight, precision=exact_mode)

def to_curve(rows_in, position):
    segments = rows_in.reshape(-1, SEG, D)
    return jnp.zeros_like(segments).at[position].set(segments).reshape(rows_in.shape)

def from_curve(rows_in, position):
    return rows_in.reshape(-1, SEG, D)[position].reshape(rows_in.shape)

def reference(points, upstream, gains, w_qkv, w_proj, z_route, h_route):
    z_position = (z_route[:, 0] * SEG_DEV + z_route[:, 1]).astype(jnp.int32)
    h_position = (h_route[:, 0] * SEG_DEV + h_route[:, 1]).astype(jnp.int32)

    def window(points, gains, w_qkv, w_proj):
        curve_first = to_curve(points, z_position)
        middle = from_curve(attend_block(curve_first, gains[0], w_qkv[0], w_proj[0]), z_position)
        curve_second = to_curve(middle, h_position)
        return from_curve(attend_block(curve_second, gains[1], w_qkv[1], w_proj[1]), h_position)
    _, pull_back = jax.vjp(window, points, gains, w_qkv, w_proj)
    point_grad, gain_grad, qkv_grad, proj_grad = pull_back(upstream)
    return (point_grad, gain_grad, qkv_grad, proj_grad)
```

```python
import math

import jax
import jax.numpy as jnp
from jax import lax
from jax.sharding import PartitionSpec as P

D = 512
HEADS = 32
PATCH = 128
SEG = 16


exact_mode = lax.Precision.HIGHEST
fast_mode = lax.Precision.HIGH
mesh_axes = ("gx", "gy")
epsilon = 1e-05


def attend_block(rows_in, gain_row, qkv_weight, proj_weight):
    row_count = rows_in.shape[0]
    head_dim = D // HEADS
    row_mean = jnp.mean(rows_in, axis=-1, keepdims=True)
    centered = rows_in - row_mean
    row_var = jnp.mean(centered * centered, axis=-1, keepdims=True)
    normed = centered * lax.rsqrt(row_var + epsilon) * gain_row
    projected = jnp.dot(normed, qkv_weight, precision=exact_mode)
    projected = projected.reshape(row_count // PATCH, PATCH, 3, HEADS, head_dim)
    queries = projected[:, :, 0]
    key_rows = projected[:, :, 1]
    value_rows = projected[:, :, 2]
    scores = jnp.einsum("pihd,pjhd->phij", queries, key_rows, precision=exact_mode) * (
        1.0 / math.sqrt(head_dim)
    )
    attention = jax.nn.softmax(scores, axis=-1)
    mixed_rows = jnp.einsum("phij,pjhd->pihd", attention, value_rows, precision=fast_mode)
    return rows_in + jnp.dot(mixed_rows.reshape(row_count, D), proj_weight, precision=fast_mode)


def occupancy(owner_index):
    count = owner_index.shape[0]
    same = owner_index[None, :] == owner_index[:, None]
    earlier = jnp.arange(count)[None, :] < jnp.arange(count)[:, None]
    return jnp.sum(same & earlier, axis=1)


def spread_out(rows_in, owner_index, dest_slot, peer_count):
    segments = rows_in.reshape(-1, SEG, rows_in.shape[1])
    seg_count = segments.shape[0]
    per_peer = seg_count // peer_count
    occur = occupancy(owner_index)
    buffer = (
        jnp.zeros((peer_count, per_peer) + segments.shape[1:], rows_in.dtype)
        .at[owner_index, occur]
        .set(segments)
    )
    labels = (
        jnp.full((peer_count, per_peer), seg_count, jnp.int32).at[owner_index, occur].set(dest_slot)
    )
    return (buffer, labels, occur)


def settle_in(received, got_labels, seg_count):
    flat = received.reshape((-1,) + received.shape[2:])
    flat_labels = got_labels.reshape(-1)
    matches = flat_labels[None, :] == jnp.arange(seg_count, dtype=jnp.int32)[:, None]
    source = jnp.sum(
        jnp.where(matches, jnp.arange(flat_labels.shape[0], dtype=jnp.int32)[None, :], 0), axis=1
    )
    return (flat[source].reshape(-1, flat.shape[2]), source)


def pack_back(rows_in, source, peer_count):
    segments = rows_in.reshape(-1, SEG, rows_in.shape[1])
    placed = jnp.zeros_like(segments).at[source].set(segments)
    return placed.reshape((peer_count, -1) + segments.shape[1:])


def to_zorder(rows_in, route):
    peer_count = lax.axis_size("gy")
    owner_index = route[:, 0] % peer_count
    buffer, labels, occur = spread_out(rows_in, owner_index, route[:, 1], peer_count)
    received, got_labels = (
        lax.all_to_all(buffer, "gy", split_axis=0, concat_axis=0, tiled=True),
        lax.all_to_all(labels, "gy", split_axis=0, concat_axis=0, tiled=True),
    )
    rows_out, source = settle_in(received, got_labels, route.shape[0])
    return (rows_out, source, occur)


def from_zorder(rows_in, source, occur, route):
    peer_count = lax.axis_size("gy")
    buffer = pack_back(rows_in, source, peer_count)
    received = lax.all_to_all(buffer, "gy", split_axis=0, concat_axis=0, tiled=True)
    return received[route[:, 0] % peer_count, occur].reshape(-1, rows_in.shape[1])


def to_hilbert(rows_in, route):
    peer_count = lax.axis_size("gx")
    owner_index = route[:, 0] // lax.axis_size("gy")
    buffer, labels, occur = spread_out(rows_in, owner_index, route[:, 1], peer_count)
    received, got_labels = (
        lax.all_to_all(buffer, "gx", split_axis=0, concat_axis=0, tiled=True),
        lax.all_to_all(labels, "gx", split_axis=0, concat_axis=0, tiled=True),
    )
    rows_out, source = settle_in(received, got_labels, route.shape[0])
    return (rows_out, source, occur)


def from_hilbert(rows_in, source, occur, route):
    peer_count = lax.axis_size("gx")
    buffer = pack_back(rows_in, source, peer_count)
    received = lax.all_to_all(buffer, "gx", split_axis=0, concat_axis=0, tiled=True)
    return received[route[:, 0] // lax.axis_size("gy"), occur].reshape(-1, rows_in.shape[1])


def halve_and_sum(part, bit_order, device_count):
    bit_count = device_count.bit_length() - 1
    me = lax.axis_index(mesh_axes)
    shaped = part.reshape((2,) * bit_count + (part.shape[0] // device_count, part.shape[1]))
    left = list(range(bit_count))
    for bit in bit_order:
        at = left.index(bit_count - 1 - bit)
        left.pop(at)
        mine = (me >> bit) & 1
        sent = lax.dynamic_index_in_dim(shaped, 1 - mine, at, keepdims=False)
        kept = lax.dynamic_index_in_dim(shaped, mine, at, keepdims=False)
        swaps = [(i, i ^ (1 << bit)) for i in range(device_count)]
        shaped = kept + lax.ppermute(sent, mesh_axes, swaps)
    return shaped


def bit_orders(mesh_gx, mesh_gy):
    gy_bits = mesh_gy.bit_length() - 1
    gx_bits = mesh_gx.bit_length() - 1
    core = gy_bits
    y_bits = list(range(gy_bits + 1, gy_bits + gx_bits))[::-1]
    low = [0]
    high = list(range(1, gy_bits))[::-1]
    return ([core] + y_bits + low + high, [core] + low + high + y_bits, [core] + high + y_bits + low)


def reduce_grads(gain_part, qkv_part, proj_part):
    mesh_gx, mesh_gy = lax.axis_size("gx"), lax.axis_size("gy")
    device_count = mesh_gx * mesh_gy
    width = qkv_part.shape[1]
    half = width // 2
    orders = bit_orders(mesh_gx, mesh_gy)
    gain_wide = jnp.broadcast_to(gain_part[:, None], (gain_part.shape[0], 128))
    proj_wide = jnp.concatenate([proj_part, gain_wide], axis=1)
    first = halve_and_sum(qkv_part[:, :half], orders[0], device_count)
    second = halve_and_sum(qkv_part[:, half:], orders[1], device_count)
    third = halve_and_sum(proj_wide, orders[2], device_count)
    qkv_sum = jnp.concatenate([first, second], axis=1)
    return (third[:, -1], qkv_sum, third[:, : proj_part.shape[1]])


def per_device(points, upstream, gains, w_qkv, w_proj, z_route, h_route):
    curve_first, z_source, z_occur = to_zorder(points, z_route)
    first_out, pull_first = jax.vjp(attend_block, curve_first, gains[0], w_qkv[0], w_proj[0])
    middle = from_zorder(first_out, z_source, z_occur, z_route)
    curve_second, h_source, h_occur = to_hilbert(middle, h_route)
    grad_curve, unused_source, unused_occur = to_hilbert(upstream, h_route)
    second_out, pull_second = jax.vjp(attend_block, curve_second, gains[1], w_qkv[1], w_proj[1])
    grad_second, gain_second, qkv_second, proj_second = pull_second(grad_curve)
    sums_second = reduce_grads(gain_second, qkv_second, proj_second)
    grad_middle = from_hilbert(grad_second, h_source, h_occur, h_route)
    middle_curve, unused_again, unused_spots = to_zorder(grad_middle, z_route)
    grad_first, gain_first, qkv_first, proj_first = pull_first(middle_curve)
    point_grad = from_zorder(grad_first, z_source, z_occur, z_route)
    sums_first = reduce_grads(gain_first, qkv_first, proj_first)
    gain_grad, qkv_grad, proj_grad = (jnp.stack(pair) for pair in zip(sums_first, sums_second))
    return (point_grad, gain_grad, qkv_grad, proj_grad)


def solution(mesh):
    return jax.shard_map(
        per_device,
        mesh=mesh,
        in_specs=(
            P(("gx", "gy"), None),
            P(("gx", "gy"), None),
            P(),
            P(),
            P(),
            P(("gx", "gy"), None),
            P(("gx", "gy"), None),
        ),
        out_specs=(
            P(("gx", "gy"), None),
            P(None, ("gx", "gy")),
            P(None, ("gx", "gy"), None),
            P(None, ("gx", "gy"), None),
        ),
        check_vma=False,
    )
```

```python
import math

import jax
import jax.numpy as jnp
from jax import lax
from jax.sharding import PartitionSpec as P

D = 512
HEADS = 32
PATCH = 128
SEG = 16


exact_mode = lax.Precision.HIGHEST
fast_mode = lax.Precision.HIGH
mesh_axes = ("gx", "gy")
epsilon = 1e-05


def project_rows(rows_in, gain_row, qkv_weight):
    row_count = rows_in.shape[0]
    row_mean = jnp.mean(rows_in, axis=-1, keepdims=True)
    centered = rows_in - row_mean
    row_var = jnp.mean(centered * centered, axis=-1, keepdims=True)
    normed = centered * lax.rsqrt(row_var + epsilon) * gain_row
    projected = jnp.dot(normed, qkv_weight, precision=exact_mode)
    return projected.reshape(row_count // PATCH, PATCH, 3, HEADS, D // HEADS)


def attend(projected):
    queries = projected[:, :, 0]
    key_rows = projected[:, :, 1]
    value_rows = projected[:, :, 2]
    scores = jnp.einsum("pihd,pjhd->phij", queries, key_rows, precision=exact_mode) * (
        1.0 / math.sqrt(D // HEADS)
    )
    attention = jax.nn.softmax(scores, axis=-1)
    return jnp.einsum("phij,pjhd->pihd", attention, value_rows, precision=fast_mode)


def leave_block(rows_in, mixed_rows, proj_weight):
    return rows_in + jnp.dot(mixed_rows.reshape(rows_in.shape), proj_weight, precision=fast_mode)


def block_forward(rows_in, gain_row, qkv_weight, proj_weight):
    projected, pull_project = jax.vjp(project_rows, rows_in, gain_row, qkv_weight)
    mixed_rows, pull_attend = jax.vjp(attend, projected)
    rows_out, pull_leave = jax.vjp(leave_block, rows_in, mixed_rows, proj_weight)
    return (rows_out, pull_project, pull_attend, pull_leave)


def occupancy(owner_index):
    count = owner_index.shape[0]
    same = owner_index[None, :] == owner_index[:, None]
    earlier = jnp.arange(count)[None, :] < jnp.arange(count)[:, None]
    return jnp.sum(same & earlier, axis=1)


def spread_out(rows_in, owner_index, dest_slot, peer_count):
    segments = rows_in.reshape(-1, SEG, rows_in.shape[1])
    seg_count = segments.shape[0]
    per_peer = seg_count // peer_count
    occur = occupancy(owner_index)
    buffer = (
        jnp.zeros((peer_count, per_peer) + segments.shape[1:], rows_in.dtype)
        .at[owner_index, occur]
        .set(segments)
    )
    labels = (
        jnp.full((peer_count, per_peer), seg_count, jnp.int32).at[owner_index, occur].set(dest_slot)
    )
    return (buffer, labels, occur)


def settle_in(received, got_labels, seg_count):
    flat = received.reshape((-1,) + received.shape[2:])
    flat_labels = got_labels.reshape(-1)
    matches = flat_labels[None, :] == jnp.arange(seg_count, dtype=jnp.int32)[:, None]
    source = jnp.sum(
        jnp.where(matches, jnp.arange(flat_labels.shape[0], dtype=jnp.int32)[None, :], 0), axis=1
    )
    return (flat[source].reshape(-1, flat.shape[2]), source)


def pack_back(rows_in, source, peer_count):
    segments = rows_in.reshape(-1, SEG, rows_in.shape[1])
    placed = jnp.zeros_like(segments).at[source].set(segments)
    return placed.reshape((peer_count, -1) + segments.shape[1:])


def to_zorder(rows_in, route):
    peer_count = lax.axis_size("gy")
    owner_index = route[:, 0] % peer_count
    buffer, labels, occur = spread_out(rows_in, owner_index, route[:, 1], peer_count)
    received, got_labels = (
        lax.all_to_all(buffer, "gy", split_axis=0, concat_axis=0, tiled=True),
        lax.all_to_all(labels, "gy", split_axis=0, concat_axis=0, tiled=True),
    )
    rows_out, source = settle_in(received, got_labels, route.shape[0])
    return (rows_out, source, occur)


def from_zorder(rows_in, source, occur, route):
    peer_count = lax.axis_size("gy")
    buffer = pack_back(rows_in, source, peer_count)
    received = lax.all_to_all(buffer, "gy", split_axis=0, concat_axis=0, tiled=True)
    return received[route[:, 0] % peer_count, occur].reshape(-1, rows_in.shape[1])


def to_hilbert(rows_in, route):
    peer_count = lax.axis_size("gx")
    owner_index = route[:, 0] // lax.axis_size("gy")
    buffer, labels, occur = spread_out(rows_in, owner_index, route[:, 1], peer_count)
    received, got_labels = (
        lax.all_to_all(buffer, "gx", split_axis=0, concat_axis=0, tiled=True),
        lax.all_to_all(labels, "gx", split_axis=0, concat_axis=0, tiled=True),
    )
    rows_out, source = settle_in(received, got_labels, route.shape[0])
    return (rows_out, source, occur)


def from_hilbert(rows_in, source, occur, route):
    peer_count = lax.axis_size("gx")
    buffer = pack_back(rows_in, source, peer_count)
    received = lax.all_to_all(buffer, "gx", split_axis=0, concat_axis=0, tiled=True)
    return received[route[:, 0] // lax.axis_size("gy"), occur].reshape(-1, rows_in.shape[1])


def pick_bits(shaped, left, bits, values, bit_count):
    left = list(left)
    for bit, value in zip(bits, values):
        at = left.index(bit_count - 1 - bit)
        left.pop(at)
        shaped = lax.dynamic_index_in_dim(shaped, value, at, keepdims=False)
    return (shaped, left)


class ScatterSum:
    def __init__(self, part, groups):
        self.device_count = lax.axis_size("gx") * lax.axis_size("gy")
        self.bit_count = self.device_count.bit_length() - 1
        self.groups = list(groups)
        self.left = list(range(self.bit_count))
        self.shaped = part.reshape(
            (2,) * self.bit_count + (part.shape[0] // self.device_count, part.shape[1])
        )
        self.kept, self.received = None, []
        self.send_next()

    def send_next(self):
        if self.received:
            self.shaped = sum(self.received, self.kept)
            self.received = []
        if not self.groups:
            return
        bits = self.groups.pop(0)
        me = lax.axis_index(mesh_axes)
        mine = [(me >> bit) & 1 for bit in bits]
        self.kept, left = pick_bits(self.shaped, self.left, bits, mine, self.bit_count)
        for flips in range(1, 1 << len(bits)):
            flip = [(flips >> i) & 1 for i in range(len(bits))]
            mask = sum(value << bit for value, bit in zip(flip, bits))
            theirs = [own ^ value for own, value in zip(mine, flip)]
            sent, unused = pick_bits(self.shaped, self.left, bits, theirs, self.bit_count)
            swaps = [(i, i ^ mask) for i in range(self.device_count)]
            self.received.append(lax.ppermute(sent, mesh_axes, swaps))
        self.left = left

    def meet(self, value):
        value, self.received = lax.optimization_barrier((value, self.received))
        self.send_next()
        return value

    def finish(self):
        while self.received:
            self.send_next()
        return self.shaped


def bit_groups(mesh_gx, mesh_gy):
    gy_bits = mesh_gy.bit_length() - 1
    gx_bits = mesh_gx.bit_length() - 1
    groups = [[gy_bits]]
    low = list(range(gy_bits // 2))
    high = list(range(gy_bits // 2, gy_bits))
    y_bits = list(range(gy_bits + 1, gy_bits + gx_bits))
    return groups + ([y_bits + low] if len(y_bits + low) < 3 else [y_bits, low]) + [high]


def with_gain(proj_part, gain_part):
    gain_wide = jnp.broadcast_to(gain_part[:, None], (gain_part.shape[0], 128))
    return jnp.concatenate([proj_part, gain_wide], axis=1)


def per_device(points, upstream, gains, w_qkv, w_proj, z_route, h_route):
    groups = bit_groups(lax.axis_size("gx"), lax.axis_size("gy"))
    wide = w_qkv.shape[2]
    tall = w_proj.shape[2]
    curve_first, z_source, z_occur = to_zorder(points, z_route)
    grad_curve, unused_source, unused_occur = to_hilbert(upstream, h_route)
    first_out, project_first, attend_first, leave_first = block_forward(
        curve_first, gains[0], w_qkv[0], w_proj[0]
    )
    middle = from_zorder(first_out, z_source, z_occur, z_route)
    curve_second, h_source, h_occur = to_hilbert(middle, h_route)
    second_out, project_second, attend_second, leave_second = block_forward(
        curve_second, gains[1], w_qkv[1], w_proj[1]
    )
    straight, grad_mixed, proj_second = leave_second(grad_curve)
    proj_sum = ScatterSum(proj_second, groups)
    (grad_projected,) = attend_second(grad_mixed)
    grad_projected = proj_sum.meet(grad_projected)
    around, gain_second, qkv_second = project_second(grad_projected)
    around = proj_sum.meet(around)
    qkv_sum = ScatterSum(with_gain(qkv_second, gain_second), groups)
    grad_middle = from_hilbert(straight + around, h_source, h_occur, h_route)
    grad_middle = proj_sum.meet(grad_middle)
    proj_second = proj_sum.finish()
    grad_middle = qkv_sum.meet(grad_middle)
    middle_curve, unused_again, unused_spots = to_zorder(grad_middle, z_route)
    straight, grad_mixed, proj_first = leave_first(middle_curve)
    grad_mixed = qkv_sum.meet(grad_mixed)
    proj_sum = ScatterSum(proj_first, groups)
    (grad_projected,) = attend_first(grad_mixed)
    grad_projected = qkv_sum.meet(grad_projected)
    grad_projected = proj_sum.meet(grad_projected)
    second_sum = qkv_sum.finish()
    around, gain_first, qkv_first = project_first(grad_projected)
    qkv_sum = ScatterSum(with_gain(qkv_first, gain_first), groups)
    point_grad = from_zorder(straight + around, z_source, z_occur, z_route)
    proj_first = proj_sum.finish()
    first_sum = qkv_sum.finish()
    return (
        point_grad,
        jnp.stack([first_sum[:, wide], second_sum[:, wide]]),
        jnp.stack([first_sum[:, :wide], second_sum[:, :wide]]),
        jnp.stack([proj_first, proj_second]),
    )


def solution(mesh):
    return jax.shard_map(
        per_device,
        mesh=mesh,
        in_specs=(
            P(("gx", "gy"), None),
            P(("gx", "gy"), None),
            P(),
            P(),
            P(),
            P(("gx", "gy"), None),
            P(("gx", "gy"), None),
        ),
        out_specs=(
            P(("gx", "gy"), None),
            P(None, ("gx", "gy")),
            P(None, ("gx", "gy"), None),
            P(None, ("gx", "gy"), None),
        ),
        check_vma=False,
    )
```

```python
import math

import jax
import jax.numpy as jnp
from jax import lax
from jax.sharding import PartitionSpec as P

D = 512
HEADS = 32
PATCH = 128
SEG = 16


exact_mode = lax.Precision.HIGHEST
fast_mode = lax.Precision.HIGH
mesh_axes = ("gx", "gy")
epsilon = 1e-05


def normalize(rows_in, gain_row):
    row_mean = jnp.mean(rows_in, axis=-1, keepdims=True)
    centered = rows_in - row_mean
    row_var = jnp.mean(centered * centered, axis=-1, keepdims=True)
    return centered * lax.rsqrt(row_var + epsilon) * gain_row


def block_forward(rows_in, gain_row, qkv_weight, proj_weight):
    row_count = rows_in.shape[0]
    normed, pull_normalize = jax.vjp(normalize, rows_in, gain_row)
    projected = jnp.dot(normed, qkv_weight, precision=exact_mode)
    heads = projected.reshape(row_count // PATCH, PATCH, 3, HEADS, D // HEADS)
    queries, key_rows, value_rows = heads[:, :, 0], heads[:, :, 1], heads[:, :, 2]
    scores = jnp.einsum("pihd,pjhd->phij", queries, key_rows, precision=exact_mode) * (
        1.0 / math.sqrt(D // HEADS)
    )
    attention = jax.nn.softmax(scores, axis=-1)
    mixed_heads = jnp.einsum("phij,pjhd->pihd", attention, value_rows, precision=fast_mode)
    mixed_rows = mixed_heads.reshape(row_count, D)
    saved = (normed, queries, key_rows, value_rows, attention, mixed_rows, pull_normalize)
    return (mixed_rows, saved)


def mixed_grads(grad_out, saved, proj_weight):
    mixed_rows = saved[5]
    grad_mixed = jnp.dot(grad_out, proj_weight.T, precision=fast_mode)
    proj_grad = jnp.dot(mixed_rows.T, grad_out, precision=fast_mode)
    return (grad_mixed, proj_grad)


def value_grads(grad_mixed, saved):
    attention = saved[4]
    grad_heads = grad_mixed.reshape(-1, PATCH, HEADS, D // HEADS)
    grad_value = jnp.einsum("phij,pihd->pjhd", attention, grad_heads, precision=fast_mode)
    return (grad_heads, grad_value.reshape(grad_mixed.shape))


def score_grads(grad_heads, saved):
    normed, queries, key_rows, value_rows, attention = saved[:5]
    grad_attention = jnp.einsum("pihd,pjhd->phij", grad_heads, value_rows, precision=fast_mode)
    along = jnp.sum(attention * grad_attention, axis=-1, keepdims=True)
    grad_scores = attention * (grad_attention - along) * (1.0 / math.sqrt(D // HEADS))
    grad_query = jnp.einsum("phij,pjhd->pihd", grad_scores, key_rows, precision=fast_mode)
    grad_key = jnp.einsum("phij,pihd->pjhd", grad_scores, queries, precision=fast_mode)
    return (grad_query.reshape(normed.shape), grad_key.reshape(normed.shape))


def weight_grad(saved, grad_projected):
    return jnp.dot(saved[0].T, grad_projected, precision=fast_mode)


def normed_grad(grad_projected, qkv_weight):
    return jnp.dot(grad_projected, qkv_weight.T, precision=fast_mode)


def occupancy(owner_index):
    count = owner_index.shape[0]
    same = owner_index[None, :] == owner_index[:, None]
    earlier = jnp.arange(count)[None, :] < jnp.arange(count)[:, None]
    return jnp.sum(same & earlier, axis=1)


def spread_out(rows_in, owner_index, dest_slot, peer_count):
    segments = rows_in.reshape(-1, SEG, rows_in.shape[1])
    seg_count = segments.shape[0]
    per_peer = seg_count // peer_count
    occur = occupancy(owner_index)
    buffer = (
        jnp.zeros((peer_count, per_peer) + segments.shape[1:], rows_in.dtype)
        .at[owner_index, occur]
        .set(segments)
    )
    labels = (
        jnp.full((peer_count, per_peer), seg_count, jnp.int32).at[owner_index, occur].set(dest_slot)
    )
    return (buffer, labels, occur)


def settle_in(received, got_labels, seg_count):
    flat = received.reshape((-1,) + received.shape[2:])
    flat_labels = got_labels.reshape(-1)
    matches = flat_labels[None, :] == jnp.arange(seg_count, dtype=jnp.int32)[:, None]
    source = jnp.sum(
        jnp.where(matches, jnp.arange(flat_labels.shape[0], dtype=jnp.int32)[None, :], 0), axis=1
    )
    return (flat[source].reshape(-1, flat.shape[2]), source)


def pack_back(rows_in, source, peer_count):
    segments = rows_in.reshape(-1, SEG, rows_in.shape[1])
    placed = jnp.zeros_like(segments).at[source].set(segments)
    return placed.reshape((peer_count, -1) + segments.shape[1:])


def to_zorder(rows_in, route):
    peer_count = lax.axis_size("gy")
    owner_index = route[:, 0] % peer_count
    buffer, labels, occur = spread_out(rows_in, owner_index, route[:, 1], peer_count)
    received, got_labels = (
        lax.all_to_all(buffer, "gy", split_axis=0, concat_axis=0, tiled=True),
        lax.all_to_all(labels, "gy", split_axis=0, concat_axis=0, tiled=True),
    )
    rows_out, source = settle_in(received, got_labels, route.shape[0])
    return (rows_out, source, occur)


def from_zorder(rows_in, source, occur, route):
    peer_count = lax.axis_size("gy")
    buffer = pack_back(rows_in, source, peer_count)
    received = lax.all_to_all(buffer, "gy", split_axis=0, concat_axis=0, tiled=True)
    return received[route[:, 0] % peer_count, occur].reshape(-1, rows_in.shape[1])


def to_hilbert(rows_in, route):
    peer_count = lax.axis_size("gx")
    owner_index = route[:, 0] // lax.axis_size("gy")
    buffer, labels, occur = spread_out(rows_in, owner_index, route[:, 1], peer_count)
    received, got_labels = (
        lax.all_to_all(buffer, "gx", split_axis=0, concat_axis=0, tiled=True),
        lax.all_to_all(labels, "gx", split_axis=0, concat_axis=0, tiled=True),
    )
    rows_out, source = settle_in(received, got_labels, route.shape[0])
    return (rows_out, source, occur)


def from_hilbert(rows_in, source, occur, route):
    peer_count = lax.axis_size("gx")
    buffer = pack_back(rows_in, source, peer_count)
    received = lax.all_to_all(buffer, "gx", split_axis=0, concat_axis=0, tiled=True)
    return received[route[:, 0] // lax.axis_size("gy"), occur].reshape(-1, rows_in.shape[1])


def pick_bits(shaped, left, bits, values, bit_count):
    left = list(left)
    for bit, value in zip(bits, values):
        at = left.index(bit_count - 1 - bit)
        left.pop(at)
        shaped = lax.dynamic_index_in_dim(shaped, value, at, keepdims=False)
    return (shaped, left)


class ScatterSum:
    def __init__(self, part, groups):
        self.device_count = lax.axis_size("gx") * lax.axis_size("gy")
        self.bit_count = self.device_count.bit_length() - 1
        self.groups = list(groups)
        self.left = list(range(self.bit_count))
        self.shaped = part.reshape(
            (2,) * self.bit_count + (part.shape[0] // self.device_count, part.shape[1])
        )
        self.kept, self.received = None, []
        self.send_next()

    def send_next(self):
        if self.received:
            self.shaped = sum(self.received, self.kept)
            self.received = []
        if not self.groups:
            return
        bits = self.groups.pop(0)
        me = lax.axis_index(mesh_axes)
        mine = [(me >> bit) & 1 for bit in bits]
        self.kept, left = pick_bits(self.shaped, self.left, bits, mine, self.bit_count)
        for flips in range(1, 1 << len(bits)):
            flip = [(flips >> i) & 1 for i in range(len(bits))]
            mask = sum(value << bit for value, bit in zip(flip, bits))
            theirs = [own ^ value for own, value in zip(mine, flip)]
            sent, unused = pick_bits(self.shaped, self.left, bits, theirs, self.bit_count)
            swaps = [(i, i ^ mask) for i in range(self.device_count)]
            self.received.append(lax.ppermute(sent, mesh_axes, swaps))
        self.left = left

    def meet(self, value):
        value, self.received = lax.optimization_barrier((value, self.received))
        self.send_next()
        return value

    def finish(self):
        while self.received:
            self.send_next()
        return self.shaped


def bit_groups(mesh_gx, mesh_gy):
    gy_bits = mesh_gy.bit_length() - 1
    gx_bits = mesh_gx.bit_length() - 1
    groups = [[gy_bits]]
    low = list(range(gy_bits // 2))
    high = list(range(gy_bits // 2, gy_bits))
    y_bits = list(range(gy_bits + 1, gy_bits + gx_bits))
    return groups + ([y_bits + low] if len(y_bits + low) < 3 else [y_bits, low]) + [high]


def with_gain(parts, gain_part):
    gain_wide = jnp.broadcast_to(gain_part[:, None], (gain_part.shape[0], 128))
    return jnp.concatenate(list(parts) + [gain_wide], axis=1)


def per_device(points, upstream, gains, w_qkv, w_proj, z_route, h_route):
    groups = bit_groups(lax.axis_size("gx"), lax.axis_size("gy"))
    wide = w_qkv.shape[2]
    tall = w_proj.shape[2]
    curve_first, z_source, z_occur = to_zorder(points, z_route)
    grad_curve, unused_source, unused_occur = to_hilbert(upstream, h_route)
    mixed_first, saved_first = block_forward(curve_first, gains[0], w_qkv[0], w_proj[0])
    mixed_out, grad_curve = lax.optimization_barrier((mixed_first, grad_curve))
    first_out = curve_first + jnp.dot(mixed_out, w_proj[0], precision=fast_mode)
    middle = from_zorder(first_out, z_source, z_occur, z_route)
    curve_second, h_source, h_occur = to_hilbert(middle, h_route)
    unused_mixed, saved_second = block_forward(curve_second, gains[1], w_qkv[1], w_proj[1])

    grad_mixed, proj_second = mixed_grads(grad_curve, saved_second, w_proj[1])
    grad_heads, grad_value = value_grads(grad_mixed, saved_second)
    grad_projected = jnp.concatenate(
        [*score_grads(grad_heads, saved_second), grad_value], axis=1
    )
    qkv_second = weight_grad(saved_second, grad_projected)
    around, gain_second = saved_second[6](normed_grad(grad_projected, w_qkv[1]))
    second_sum = ScatterSum(with_gain([qkv_second, proj_second], gain_second), groups)

    grad_middle = from_hilbert(grad_curve + around, h_source, h_occur, h_route)
    grad_middle = second_sum.meet(grad_middle)
    middle_curve, unused_again, unused_spots = to_zorder(grad_middle, z_route)
    grad_mixed, proj_first = mixed_grads(middle_curve, saved_first, w_proj[0])
    grad_heads, grad_value = value_grads(grad_mixed, saved_first)
    grad_heads = second_sum.meet(grad_heads)
    value_first = weight_grad(saved_first, grad_value)
    early_sum = ScatterSum(jnp.concatenate([value_first, proj_first], axis=1), groups)
    grad_query, grad_key = score_grads(grad_heads, saved_first)
    grad_pair = jnp.concatenate([grad_query, grad_key], axis=1)
    grad_pair = second_sum.meet(grad_pair)
    grad_pair = early_sum.meet(grad_pair)
    second = second_sum.finish()
    grad_normed = normed_grad(jnp.concatenate([grad_pair, grad_value], axis=1), w_qkv[0])
    around, gain_first = saved_first[6](grad_normed)
    late_sum = ScatterSum(with_gain([weight_grad(saved_first, grad_pair)], gain_first), groups)
    point_grad = from_zorder(middle_curve + around, z_source, z_occur, z_route)
    early = early_sum.finish()
    late = late_sum.finish()
    pair_wide = wide - tall
    qkv_first = jnp.concatenate([late[:, :pair_wide], early[:, :tall]], axis=1)
    return (
        point_grad,
        jnp.stack([late[:, pair_wide], second[:, wide + tall]]),
        jnp.stack([qkv_first, second[:, :wide]]),
        jnp.stack([early[:, tall:], second[:, wide : wide + tall]]),
    )


def solution(mesh):
    return jax.shard_map(
        per_device,
        mesh=mesh,
        in_specs=(
            P(("gx", "gy"), None),
            P(("gx", "gy"), None),
            P(),
            P(),
            P(),
            P(("gx", "gy"), None),
            P(("gx", "gy"), None),
        ),
        out_specs=(
            P(("gx", "gy"), None),
            P(None, ("gx", "gy")),
            P(None, ("gx", "gy"), None),
            P(None, ("gx", "gy"), None),
        ),
        check_vma=False,
    )
```

```python
import math

import jax
import jax.numpy as jnp
from jax import lax
from jax.sharding import PartitionSpec as P

D = 512
HEADS = 32
PATCH = 128
SEG = 16


exact_mode = lax.Precision.HIGHEST
fast_mode = lax.Precision.HIGH
mesh_axes = ("gx", "gy")
epsilon = 1e-05


def normalize(rows_in, gain_row):
    row_mean = jnp.mean(rows_in, axis=-1, keepdims=True)
    centered = rows_in - row_mean
    row_var = jnp.mean(centered * centered, axis=-1, keepdims=True)
    return centered * lax.rsqrt(row_var + epsilon) * gain_row


def block_forward(rows_in, gain_row, qkv_weight, proj_weight):
    row_count = rows_in.shape[0]
    normed, pull_normalize = jax.vjp(normalize, rows_in, gain_row)
    projected = jnp.dot(normed, qkv_weight, precision=exact_mode)
    heads = projected.reshape(row_count // PATCH, PATCH, 3, HEADS, D // HEADS)
    queries, key_rows, value_rows = heads[:, :, 0], heads[:, :, 1], heads[:, :, 2]
    scores = jnp.einsum("pihd,pjhd->phij", queries, key_rows, precision=exact_mode) * (
        1.0 / math.sqrt(D // HEADS)
    )
    attention = jax.nn.softmax(scores, axis=-1)
    mixed_heads = jnp.einsum("phij,pjhd->pihd", attention, value_rows, precision=fast_mode)
    mixed_rows = mixed_heads.reshape(row_count, D)
    saved = (normed, queries, key_rows, value_rows, attention, mixed_rows, pull_normalize)
    return (mixed_rows, saved)


def mixed_grads(grad_out, saved, proj_weight):
    mixed_rows = saved[5]
    grad_mixed = jnp.dot(grad_out, proj_weight.T, precision=fast_mode)
    proj_grad = jnp.dot(mixed_rows.T, grad_out, precision=fast_mode)
    return (grad_mixed, proj_grad)


def value_grads(grad_mixed, saved):
    attention = saved[4]
    grad_heads = grad_mixed.reshape(-1, PATCH, HEADS, D // HEADS)
    grad_value = jnp.einsum("phij,pihd->pjhd", attention, grad_heads, precision=fast_mode)
    return (grad_heads, grad_value.reshape(grad_mixed.shape))


def score_grads(grad_heads, saved):
    normed, queries, key_rows, value_rows, attention = saved[:5]
    grad_attention = jnp.einsum("pihd,pjhd->phij", grad_heads, value_rows, precision=fast_mode)
    along = jnp.sum(attention * grad_attention, axis=-1, keepdims=True)
    grad_scores = attention * (grad_attention - along) * (1.0 / math.sqrt(D // HEADS))
    grad_query = jnp.einsum("phij,pjhd->pihd", grad_scores, key_rows, precision=fast_mode)
    grad_key = jnp.einsum("phij,pihd->pjhd", grad_scores, queries, precision=fast_mode)
    return (grad_query.reshape(normed.shape), grad_key.reshape(normed.shape))


def weight_grad(saved, grad_projected):
    return jnp.dot(saved[0].T, grad_projected, precision=fast_mode)


def normed_grad(grad_projected, qkv_weight):
    return jnp.dot(grad_projected, qkv_weight.T, precision=fast_mode)


def occupancy(owner_index):
    count = owner_index.shape[0]
    same = owner_index[None, :] == owner_index[:, None]
    earlier = jnp.arange(count)[None, :] < jnp.arange(count)[:, None]
    return jnp.sum(same & earlier, axis=1)


def spread_out(rows_in, owner_index, dest_slot, peer_count):
    segments = rows_in.reshape(-1, SEG, rows_in.shape[1])
    seg_count = segments.shape[0]
    per_peer = seg_count // peer_count
    occur = occupancy(owner_index)
    buffer = (
        jnp.zeros((peer_count, per_peer) + segments.shape[1:], rows_in.dtype)
        .at[owner_index, occur]
        .set(segments)
    )
    labels = (
        jnp.full((peer_count, per_peer), seg_count, jnp.int32).at[owner_index, occur].set(dest_slot)
    )
    return (buffer, labels, occur)


def settle_in(received, got_labels, seg_count):
    flat = received.reshape((-1,) + received.shape[2:])
    flat_labels = got_labels.reshape(-1)
    matches = flat_labels[None, :] == jnp.arange(seg_count, dtype=jnp.int32)[:, None]
    source = jnp.sum(
        jnp.where(matches, jnp.arange(flat_labels.shape[0], dtype=jnp.int32)[None, :], 0), axis=1
    )
    return (flat[source].reshape(-1, flat.shape[2]), source)


def pack_back(rows_in, source, peer_count):
    segments = rows_in.reshape(-1, SEG, rows_in.shape[1])
    placed = jnp.zeros_like(segments).at[source].set(segments)
    return placed.reshape((peer_count, -1) + segments.shape[1:])


def to_zorder(rows_in, route):
    peer_count = lax.axis_size("gy")
    owner_index = route[:, 0] % peer_count
    buffer, labels, occur = spread_out(rows_in, owner_index, route[:, 1], peer_count)
    received, got_labels = (
        lax.all_to_all(buffer, "gy", split_axis=0, concat_axis=0, tiled=True),
        lax.all_to_all(labels, "gy", split_axis=0, concat_axis=0, tiled=True),
    )
    rows_out, source = settle_in(received, got_labels, route.shape[0])
    return (rows_out, source, occur)


def from_zorder(rows_in, source, occur, route):
    peer_count = lax.axis_size("gy")
    buffer = pack_back(rows_in, source, peer_count)
    received = lax.all_to_all(buffer, "gy", split_axis=0, concat_axis=0, tiled=True)
    return received[route[:, 0] % peer_count, occur].reshape(-1, rows_in.shape[1])


def to_hilbert(rows_in, route):
    peer_count = lax.axis_size("gx")
    owner_index = route[:, 0] // lax.axis_size("gy")
    buffer, labels, occur = spread_out(rows_in, owner_index, route[:, 1], peer_count)
    received, got_labels = (
        lax.all_to_all(buffer, "gx", split_axis=0, concat_axis=0, tiled=True),
        lax.all_to_all(labels, "gx", split_axis=0, concat_axis=0, tiled=True),
    )
    rows_out, source = settle_in(received, got_labels, route.shape[0])
    return (rows_out, source, occur)


def from_hilbert(rows_in, source, occur, route):
    peer_count = lax.axis_size("gx")
    buffer = pack_back(rows_in, source, peer_count)
    received = lax.all_to_all(buffer, "gx", split_axis=0, concat_axis=0, tiled=True)
    return received[route[:, 0] // lax.axis_size("gy"), occur].reshape(-1, rows_in.shape[1])


def pick_bits(shaped, left, bits, values, bit_count):
    left = list(left)
    for bit, value in zip(bits, values):
        at = left.index(bit_count - 1 - bit)
        left.pop(at)
        shaped = lax.dynamic_index_in_dim(shaped, value, at, keepdims=False)
    return (shaped, left)


class ScatterSum:
    def __init__(self, part, groups):
        self.device_count = lax.axis_size("gx") * lax.axis_size("gy")
        self.bit_count = self.device_count.bit_length() - 1
        self.groups = list(groups)
        self.left = list(range(self.bit_count))
        self.shaped = part.reshape(
            (2,) * self.bit_count + (part.shape[0] // self.device_count, part.shape[1])
        )
        self.kept, self.received = None, []
        self.send_next()

    def send_next(self):
        if self.received:
            self.shaped = sum(self.received, self.kept)
            self.received = []
        if not self.groups:
            return
        bits = self.groups.pop(0)
        me = lax.axis_index(mesh_axes)
        mine = [(me >> bit) & 1 for bit in bits]
        self.kept, left = pick_bits(self.shaped, self.left, bits, mine, self.bit_count)
        for flips in range(1, 1 << len(bits)):
            flip = [(flips >> i) & 1 for i in range(len(bits))]
            mask = sum(value << bit for value, bit in zip(flip, bits))
            theirs = [own ^ value for own, value in zip(mine, flip)]
            sent, unused = pick_bits(self.shaped, self.left, bits, theirs, self.bit_count)
            swaps = [(i, i ^ mask) for i in range(self.device_count)]
            self.received.append(lax.ppermute(sent, mesh_axes, swaps))
        self.left = left

    def meet(self, value):
        value, self.received = lax.optimization_barrier((value, self.received))
        self.send_next()
        return value

    def finish(self):
        while self.received:
            self.send_next()
        return self.shaped


def bit_groups(mesh_gx, mesh_gy):
    gy_bits = mesh_gy.bit_length() - 1
    gx_bits = mesh_gx.bit_length() - 1
    groups = [[gy_bits]]
    low = list(range(gy_bits // 2))
    high = list(range(gy_bits // 2, gy_bits))
    y_bits = list(range(gy_bits + 1, gy_bits + gx_bits))
    return groups + ([y_bits + low] if len(y_bits + low) < 3 else [y_bits, low]) + [high]


def with_gain(parts, gain_part):
    gain_wide = jnp.broadcast_to(gain_part[:, None], (gain_part.shape[0], 128))
    return jnp.concatenate(list(parts) + [gain_wide], axis=1)


def per_device(points, upstream, gains, w_qkv, w_proj, z_route, h_route):
    groups = bit_groups(lax.axis_size("gx"), lax.axis_size("gy"))
    wide = w_qkv.shape[2]
    tall = w_proj.shape[2]
    curve_first, z_source, z_occur = to_zorder(points, z_route)
    grad_curve, unused_source, unused_occur = to_hilbert(upstream, h_route)
    mixed_first, saved_first = block_forward(curve_first, gains[0], w_qkv[0], w_proj[0])
    first_out = curve_first + jnp.dot(mixed_first, w_proj[0], precision=fast_mode)
    middle = from_zorder(first_out, z_source, z_occur, z_route)
    curve_second, h_source, h_occur = to_hilbert(middle, h_route)
    unused_mixed, saved_second = block_forward(curve_second, gains[1], w_qkv[1], w_proj[1])

    grad_mixed, proj_second = mixed_grads(grad_curve, saved_second, w_proj[1])
    grad_heads, grad_value = value_grads(grad_mixed, saved_second)
    grad_projected = jnp.concatenate(
        [*score_grads(grad_heads, saved_second), grad_value], axis=1
    )
    qkv_second = weight_grad(saved_second, grad_projected)
    around, gain_second = saved_second[6](normed_grad(grad_projected, w_qkv[1]))
    second_sum = ScatterSum(with_gain([qkv_second, proj_second], gain_second), groups)

    grad_middle = from_hilbert(grad_curve + around, h_source, h_occur, h_route)
    grad_middle = second_sum.meet(grad_middle)
    middle_curve, unused_again, unused_spots = to_zorder(grad_middle, z_route)
    grad_mixed, proj_first = mixed_grads(middle_curve, saved_first, w_proj[0])
    grad_heads, grad_value = value_grads(grad_mixed, saved_first)
    value_first = weight_grad(saved_first, grad_value)
    early_sum = ScatterSum(jnp.concatenate([value_first, proj_first], axis=1), groups)
    grad_query, grad_key = score_grads(grad_heads, saved_first)
    grad_pair = jnp.concatenate([grad_query, grad_key], axis=1)
    grad_pair = second_sum.meet(grad_pair)
    grad_pair = early_sum.meet(grad_pair)
    grad_normed = normed_grad(jnp.concatenate([grad_pair, grad_value], axis=1), w_qkv[0])
    grad_normed = second_sum.meet(grad_normed)
    second = second_sum.finish()
    around, gain_first = saved_first[6](grad_normed)
    late_sum = ScatterSum(with_gain([weight_grad(saved_first, grad_pair)], gain_first), groups)
    point_grad = from_zorder(middle_curve + around, z_source, z_occur, z_route)
    early = early_sum.finish()
    late = late_sum.finish()
    pair_wide = wide - tall
    qkv_first = jnp.concatenate([late[:, :pair_wide], early[:, :tall]], axis=1)
    return (
        point_grad,
        jnp.stack([late[:, pair_wide], second[:, wide + tall]]),
        jnp.stack([qkv_first, second[:, :wide]]),
        jnp.stack([early[:, tall:], second[:, wide : wide + tall]]),
    )


def solution(mesh):
    return jax.shard_map(
        per_device,
        mesh=mesh,
        in_specs=(
            P(("gx", "gy"), None),
            P(("gx", "gy"), None),
            P(),
            P(),
            P(),
            P(("gx", "gy"), None),
            P(("gx", "gy"), None),
        ),
        out_specs=(
            P(("gx", "gy"), None),
            P(None, ("gx", "gy")),
            P(None, ("gx", "gy"), None),
            P(None, ("gx", "gy"), None),
        ),
        check_vma=False,
    )
```
